32 devices in a mesh: ctx: 8 (over z, core), head: 4 (over y, x).
Axes of the slice: x: 2, y: 2, z: 4, core: 2. Of those that a mesh axis runs over, the one named last changes fastest.
Arguments:
- query: bfloat16 [2048, 32, 128], P(('ctx', 'head')), may hold values from -6 to 6
- key: bfloat16 [2048, 16, 128], P(('ctx', 'head')), may hold values from -6 to 6
- value: bfloat16 [2048, 16, 128], P(('ctx', 'head')), may hold values from -6 to 6
- attn_out: bfloat16 [2048, 32, 128], P('ctx', 'head'), may hold values from -6 to 6
- out_grad: bfloat16 [2048, 32, 128], P(('ctx', 'head')), may hold values from -4 to 4
- lse: bfloat16 [32, 2048], P('head', 'ctx'), may hold values from 3 to 5
- doc_lengths: int32 [8], replicated, may hold values from 1 to 512, 2048 in all
Outputs:
- query_grad: bfloat16 [2048, 32, 128], P(('ctx', 'head'))
- key_grad: bfloat16 [2048, 16, 128], P(('ctx', 'head'))
- value_grad: bfloat16 [2048, 16, 128], P(('ctx', 'head'))
The draws below stay inside these ranges and needn't reach their ends.
Inputs may be any that keep to these rules, and one draw needn't show every extreme that they name: `doc_lengths`: document lengths in the order of the packed sequence; they sum to 2048 and the largest is exactly 512.
All inputs are finite; a program needn't handle non-finite values.
Results may differ from the reference program's by a relative error of at most 0.0053.
Values may be sent and summed in bfloat16 or wider, within the bound.
No kernel may reach another device: no remote copies, remote signals or barrier semaphores. Data moves between devices by JAX's collectives and lax.ppermute only.
A program may use at most 64 MiB of HBM per device.

```python
import math
import jax
import jax.numpy as jnp
import numpy as np
from jax import lax

HD = 128
QH = 32
KVH = 16
TOK_DEV = 256
REACH = 2
SEQ = 2048
MOST = 512
NDOCS = 8


def block_scale(key, extent, pieces, smallest, top_value):
    def one(axis_at, shards_of):
        heights = jax.random.uniform(jax.random.fold_in(jax.random.fold_in(key, 6), axis_at), (shards_of,), jnp.float32, smallest / len(pieces), top_value / len(pieces))
        return jnp.repeat(jnp.exp(heights), extent[axis_at] // shards_of).reshape((-1,) + (1,) * (len(extent) - axis_at - 1))

    factor_of = one(*pieces[0])
    for cut in pieces[1:]:
        factor_of = factor_of * one(*cut)
    return factor_of


def length_profile(amount, total, reach, skew):
    weights = [(1 << 20) // math.isqrt(grade ** skew) + 1 for grade in range(2, amount + 1)]
    surplus, holding = total - reach - (amount - 1), [1] * (amount - 1)
    while surplus > 0:
        free = [i for i in range(amount - 1) if holding[i] < reach]
        whole, remaining = sum([weights[i] for i in free]), surplus
        for i in free:
            more = min(reach - holding[i], max(1, remaining * weights[i] // whole), surplus)
            holding[i] = holding[i] + more
            surplus = surplus - more
    return np.array([reach] + holding)


def ragged_sizes(rng, amount, total, limit, skew):
    if amount == 2:
        one = jax.random.randint(rng, (), max(1, total - limit), min(limit, total - 1) + 1)
        return jnp.stack([one, total - one])
    sizes = jnp.asarray(length_profile(amount, total, limit, skew), jnp.int32)
    pairs = (amount - 1) // 2
    donor, sink = sizes[1:1 + 2 * pairs:2], sizes[2:2 + 2 * pairs:2]
    margin = jnp.minimum(donor - 1, limit - sink)
    passed = jax.random.randint(jax.random.fold_in(rng, 1), (pairs,), 0, 1 << 20) % (margin + 1)
    sizes = sizes.at[1:1 + 2 * pairs:2].set(donor - passed).at[2:2 + 2 * pairs:2].set(sink + passed)
    return sizes[jax.random.permutation(jax.random.fold_in(rng, 2), amount)]


def gaussian(rng, shape, width, reach, pieces=(), held_as=jnp.bfloat16):
    drawn = width * jax.random.normal(rng, shape, jnp.float32)
    if pieces:
        drawn = drawn * block_scale(rng, shape, pieces, -0.22, 0.18)
    return jnp.clip(drawn, -reach, reach).astype(held_as)


def setup_inputs(seed: int = 0) -> dict:
    key_list = jax.random.split(jax.random.key(seed), 8)
    query = gaussian(key_list[0], (SEQ, QH, HD), (14.4 ** 0.5 * HD ** -0.25), 6.0, ((0, 32),))
    key = gaussian(key_list[1], (SEQ, KVH, HD), (14.4 ** 0.5 * HD ** -0.25), 6.0, ((0, 32),))
    value = gaussian(key_list[2], (SEQ, KVH, HD), 1.0, 6.0, ((0, 32),))
    attn_out = gaussian(key_list[3], (SEQ, QH, HD), 1.0, 6.0, ((0, 8), (1, 4)))
    out_grad = gaussian(key_list[4], (SEQ, QH, HD), (3.0 * HD ** -0.5), 4.0, ((0, 32),))
    lse = jnp.clip(3.0 + 2.0 * jax.random.uniform(key_list[5], (QH, SEQ), jnp.float32) ** block_scale(key_list[5], (QH, SEQ), ((0, 4), (1, 8)), -0.2, 0.2), 3.0, 5.0).astype(jnp.bfloat16)
    doc_lengths = ragged_sizes(key_list[6], NDOCS, SEQ, MOST, 2).astype(jnp.int32)
    return dict(query=query, key=key, value=value, attn_out=attn_out, out_grad=out_grad, lse=lse, doc_lengths=doc_lengths)


soft_cap = 50.0
score_scale = 144.0 ** -0.5


def doc_index(positions, doc_ends):
    return jnp.sum((positions[:, None] >= doc_ends[None, :]).astype(jnp.int32), axis=1).astype(jnp.int32)


def block_grads(queries, out_grads, lse_rows, delta_rows, key_rows, value_rows, allowed):
    q_full = queries.astype(jnp.float32)
    g_full = out_grads.astype(jnp.float32)
    k_full = key_rows.astype(jnp.float32)
    v_full = value_rows.astype(jnp.float32)
    raw_scores = jnp.einsum("tkgd,ukd->kgtu", q_full, k_full)
    capped = soft_cap * jnp.tanh(raw_scores * (score_scale / soft_cap))
    weights = jnp.where(allowed[None, None], jnp.exp(capped - lse_rows[..., None]), 0.0)
    d_weights = jnp.einsum("tkgd,ukd->kgtu", g_full, v_full)
    d_scores = (weights * (d_weights - delta_rows[..., None]) * (1.0 - (capped / soft_cap) ** 2) * score_scale).astype(jnp.bfloat16)
    weights_low = weights.astype(jnp.bfloat16)
    ds_full = d_scores.astype(jnp.float32)
    w_full = weights_low.astype(jnp.float32)
    d_query = jnp.einsum("kgtu,ukd->tkgd", ds_full, k_full)
    d_key = jnp.einsum("kgtu,tkgd->ukd", ds_full, q_full)
    d_value = jnp.einsum("kgtu,tkgd->ukd", w_full, g_full)
    return d_query, d_key, d_value


def reference(query, key, value, attn_out, out_grad, lse, doc_lengths):
    per_group = QH // KVH
    q_tokens = query.reshape(SEQ, KVH, per_group, HD)
    g_tokens = out_grad.reshape(SEQ, KVH, per_group, HD)
    o_tokens = attn_out.reshape(SEQ, KVH, per_group, HD)
    lse_all = lse.astype(jnp.float32).reshape(KVH, per_group, SEQ)
    delta_all = jnp.transpose(jnp.sum(g_tokens.astype(jnp.float32) * o_tokens.astype(jnp.float32), axis=-1), (1, 2, 0))
    doc_ends = jnp.cumsum(doc_lengths).astype(jnp.int32)
    span = REACH * TOK_DEV
    window = span + TOK_DEV
    zero_rows = jnp.zeros((span, KVH, HD), key.dtype)
    keys_padded = jnp.concatenate([zero_rows, key], axis=0)
    values_padded = jnp.concatenate([zero_rows, value], axis=0)

    def one_block(totals, block_index):
        first_row = (block_index * TOK_DEV).astype(jnp.int32)
        q_block = lax.dynamic_slice_in_dim(q_tokens, first_row, TOK_DEV, 0)
        g_block = lax.dynamic_slice_in_dim(g_tokens, first_row, TOK_DEV, 0)
        lse_block = lax.dynamic_slice_in_dim(lse_all, first_row, TOK_DEV, 2)
        delta_block = lax.dynamic_slice_in_dim(delta_all, first_row, TOK_DEV, 2)
        k_window = lax.dynamic_slice_in_dim(keys_padded, first_row, window, 0)
        v_window = lax.dynamic_slice_in_dim(values_padded, first_row, window, 0)
        q_pos = first_row + jnp.arange(TOK_DEV, dtype=jnp.int32)
        k_pos = first_row - span + jnp.arange(window, dtype=jnp.int32)
        allowed = (doc_index(q_pos, doc_ends)[:, None] == doc_index(k_pos, doc_ends)[None, :]) & (k_pos[None, :] <= q_pos[:, None]) & (k_pos[None, :] >= 0)
        d_query, d_key, d_value = block_grads(q_block, g_block, lse_block, delta_block, k_window, v_window, allowed)
        key_grads = jnp.stack([d_key, d_value], axis=1)
        previous = lax.dynamic_slice_in_dim(totals, first_row, window, 0)
        totals = lax.dynamic_update_slice_in_dim(totals, previous + key_grads, first_row, 0)
        return totals, d_query.astype(jnp.bfloat16)

    totals = jnp.zeros((SEQ + span, 2, KVH, HD), jnp.float32)
    totals, dq_blocks = lax.scan(one_block, totals, jnp.arange(SEQ // TOK_DEV, dtype=jnp.int32))
    query_grad = dq_blocks.reshape(SEQ, QH, HD)
    kv_grads = totals[span:].astype(jnp.bfloat16)
    return (query_grad, kv_grads[:, 0], kv_grads[:, 1])
```

```python
import functools
import math

import jax
import jax.numpy as jnp
from jax import lax
from jax.experimental import pallas as pl
from jax.experimental.pallas import tpu as pltpu
from jax.sharding import PartitionSpec as P

soft_cap = 50.0
score_scale = 144.0 ** (-0.5)
log2e = math.log2(math.e)


def swap_heads(value, step):
    count = lax.axis_size("head")
    return lax.ppermute(value, "head", [(i, i ^ step) for i in range(count)])


def rotate_ctx(value, steps):
    count = lax.axis_size("ctx")
    return lax.ppermute(value, "ctx", [(i, (i + steps) % count) for i in range(count)])


def swap_cores(value):
    count = lax.axis_size("ctx")
    return lax.ppermute(value, "ctx", [(i, i ^ 1) for i in range(count)])


def xor_order(blocks, index):
    count = blocks.shape[0]
    step = 1
    while step < count:
        swapped = blocks.reshape((count // (2 * step), 2, step) + blocks.shape[1:])[:, ::-1].reshape(blocks.shape)
        blocks = jnp.where((index & step) != 0, swapped, blocks)
        step *= 2
    return blocks


def dot(a, b, contract):
    return lax.dot_general(a, b, ((contract[0], contract[1]), ((), ())), preferred_element_type=jnp.float32)


NT = ((1,), (1,))
NN = ((1,), (0,))


def grads_kernel(planes, far, group, n_pieces, *refs):
    refs = list(refs)

    def take(n):
        out = refs[:n]
        del refs[:n]
        return out

    own_q, other_q = take(n_pieces), take(n_pieces)
    kv = [take(n_pieces) for _ in range(planes + 1)]
    own_o, other_o, own_lse, other_lse, own_start, other_start = take(6)
    dq_own, dq_other = take(n_pieces), take(n_pieces)
    dkv = [take(n_pieces) for _ in range(planes + 1)]
    acc_kv, acc_dq, ds_ref = take(3)

    rows, width = own_q[0].shape[2], own_q[0].shape[3]
    keys = rows * n_pieces
    ctx = lax.axis_index("ctx")
    head = lax.axis_index("head")
    core = ctx & 1

    acc_kv[...] = jnp.zeros_like(acc_kv)
    acc_dq[...] = jnp.zeros_like(acc_dq)

    def load_q(pieces, which):
        return jnp.concatenate([pieces[p][which, g] for g in range(group) for p in range(n_pieces)], axis=0)

    lane = lax.broadcasted_iota(jnp.int32, (1, group * keys), 1) % keys
    in_block = ((lane // rows) ^ head) * rows + lane % rows

    q_sets = []
    for pieces, o_ref, lse_ref, start_ref in (
        (own_q, own_o, own_lse, own_start),
        (other_q, other_o, other_lse, other_start),
    ):
        q_rows, g_rows = load_q(pieces, 0), load_q(pieces, 1)
        o_rows = o_ref[...].reshape(group * keys, width)
        prod = g_rows.astype(jnp.float32) * o_rows.astype(jnp.float32)
        high = prod.astype(jnp.bfloat16)
        low = (prod - high.astype(jnp.float32)).astype(jnp.bfloat16)
        ones = jnp.ones((8, width), jnp.bfloat16)
        delta = (dot(ones, high, NT) + dot(ones, low, NT))[0:1]
        q_sets.append((q_rows, g_rows, delta, lse_ref[0] * log2e, start_ref[...]))

    def pair(which_q, plane):
        q_rows, g_rows, delta, lse2, start = q_sets[which_q]
        key_ctx = ctx - 2 * plane
        for p in range(n_pieces):
            k_rows, v_rows = kv[plane][p][0, 0], kv[plane][p][1, 0]
            k_pos = key_ctx * keys + (head ^ p) * rows + lax.broadcasted_iota(jnp.int32, (rows, 1), 0)
            scores = dot(k_rows, q_rows, NT)
            d_weights = dot(v_rows, g_rows, NT)
            t = jnp.tanh(scores * (score_scale / soft_cap))
            weights = jnp.exp2(t * (soft_cap * log2e) - lse2)
            allowed = k_pos >= start
            if which_q == 0 and plane == 0:
                allowed = allowed & (k_pos <= ctx * keys + in_block)
            weights = jnp.where(allowed, weights, 0.0)
            d_scores = weights * (d_weights - delta) * ((1.0 - t * t) * score_scale)
            d_scores = d_scores.astype(jnp.bfloat16)
            ds_ref[pl.ds(p * rows, rows)] = d_scores
            span = pl.ds(p * rows, rows)
            acc_kv[plane, 0, span] += dot(d_scores, q_rows, NN)
            acc_kv[plane, 1, span] += dot(weights.astype(jnp.bfloat16), g_rows, NN)
        k_all = jnp.concatenate([kv[plane][p][0, 0] for p in range(n_pieces)], axis=0)
        acc_dq[which_q] += dot(k_all.T, ds_ref[...], NN)

    for plane in range(planes + 1):
        pair(0, plane)
        reached = ((core == 0) & (2 * plane + 1 <= far)) | ((core == 1) & (plane >= 1))
        pl.when(reached)(functools.partial(pair, 1, plane))

    for which_q, outs in ((0, dq_own), (1, dq_other)):
        full = acc_dq[which_q].T.reshape(group, n_pieces, rows, width)
        for p in range(n_pieces):
            outs[p][...] = full[:, p].astype(outs[p].dtype)
    for plane in range(planes + 1):
        for p in range(n_pieces):
            span = pl.ds(p * rows, rows)
            for which in range(2):
                dkv[plane][p][which, 0] = acc_kv[plane, which, span].astype(dkv[plane][p].dtype)


def grads_call(planes, far, group, own_q, other_q, kv, o_pair, lse_pair, start_pair):
    n_pieces = len(own_q)
    _, heads, rows, width = own_q[0].shape
    kv_heads = heads // group
    keys = rows * n_pieces
    f32, bf16 = jnp.float32, jnp.bfloat16
    q_spec = pl.BlockSpec((2, group, rows, width), lambda i: (0, i, 0, 0))
    kv_spec = pl.BlockSpec((2, 1, rows, width), lambda i: (0, i, 0, 0))
    o_spec = pl.BlockSpec((group, keys, width), lambda i: (i, 0, 0))
    lse_spec = pl.BlockSpec((1, 1, group * keys), lambda i: (i, 0, 0))
    start_spec = pl.BlockSpec((1, group * keys), lambda i: (0, 0))
    dq_spec = pl.BlockSpec((group, rows, width), lambda i: (i, 0, 0))
    shape = jax.ShapeDtypeStruct
    dq_shape, kv_shape = (heads, rows, width), (2, kv_heads, rows, width)
    pairs = kv_heads * 3 * planes * group
    outs = pl.pallas_call(
        functools.partial(grads_kernel, planes, far, group, n_pieces),
        grid=(kv_heads,),
        in_specs=[q_spec] * (2 * n_pieces) + [kv_spec] * ((planes + 1) * n_pieces) + [o_spec] * 2 + [lse_spec] * 2 + [start_spec] * 2,
        out_specs=[dq_spec] * (2 * n_pieces) + [kv_spec] * ((planes + 1) * n_pieces),
        out_shape=[shape(dq_shape, f32)] * n_pieces
        + [shape(dq_shape, bf16)] * n_pieces
        + [shape(kv_shape, f32)] * n_pieces
        + [shape(kv_shape, bf16)] * (planes * n_pieces),
        scratch_shapes=[
            pltpu.VMEM((planes + 1, 2, keys, width), f32),
            pltpu.VMEM((2, width, group * keys), f32),
            pltpu.VMEM((keys, group * keys), bf16),
        ],
        compiler_params=pltpu.CompilerParams(dimension_semantics=("arbitrary",), vmem_limit_bytes=24 * 1024 * 1024),
        cost_estimate=pl.CostEstimate(
            flops=pairs * 10 * keys * keys * width, bytes_accessed=8 * 1024 * 1024, transcendentals=pairs * 2 * keys * keys
        ),
        name="grads",
    )(*own_q, *other_q, *[piece for plane in kv for piece in plane], *o_pair, *lse_pair, *start_pair)
    chunks = [outs[i : i + n_pieces] for i in range(0, len(outs), n_pieces)]
    return chunks[0], chunks[1], chunks[2], chunks[3:]


def per_device(query, key, value, attn_out, out_grad, lse, doc_lengths):
    n_ctx, n_head = lax.axis_size("ctx"), lax.axis_size("head")
    far = min(6, n_ctx // 4)
    planes = (far + 1) // 2
    rows, heads_all, width = query.shape
    kv_all = key.shape[1]
    group = heads_all // kv_all
    ctx, head = lax.axis_index("ctx"), lax.axis_index("head")

    def piece(arrays, p):
        parts = []
        for x in arrays:
            blocks = x.reshape(rows, n_head, x.shape[1] // n_head, width)
            part = lax.dynamic_index_in_dim(blocks, head ^ p, 1, keepdims=False)
            parts.append(jnp.transpose(part, (1, 0, 2)))
        return jnp.stack(parts)

    kv_send = [piece((key, value), p) for p in range(n_head)]
    q_send = [piece((query, out_grad), p) for p in range(n_head)]
    exchange = lambda pieces: [pieces[0]] + [swap_heads(pieces[p], p) for p in range(1, n_head)]
    kv_own = exchange(kv_send)
    q_own = exchange(q_send)
    kv = [kv_own]
    for _ in range(planes):
        kv.append([rotate_ctx(piece_, 2) for piece_ in kv[-1]])
    q_other = [swap_cores(piece_) for piece_ in q_own]

    tok = rows * n_head
    heads_here = attn_out.shape[1]
    o_blocks = xor_order(attn_out.reshape(n_head, rows, heads_here, width), head)
    o_own = jnp.transpose(o_blocks, (2, 0, 1, 3)).reshape(heads_here, tok, width)
    o_other = swap_cores(o_own)
    lse_blocks = xor_order(jnp.transpose(lse.reshape(heads_here, n_head, rows), (1, 0, 2)), head)
    lse_own = jnp.transpose(lse_blocks, (1, 0, 2)).reshape(heads_here // group, 1, group * tok)
    lse_other = swap_cores(lse_own)

    doc_ends = jnp.cumsum(doc_lengths)

    def first_of_doc(block):
        lane = jnp.arange(tok, dtype=jnp.int32)
        pos = block * tok + ((lane // rows) ^ head) * rows + lane % rows
        start = jnp.max(jnp.where(doc_ends[None, :] <= pos[:, None], doc_ends[None, :], 0), axis=1)
        return jnp.tile(start, group)[None]

    dq_own, dq_other, dkv_own, dkv_far = grads_call(
        planes, far, group, q_own, q_other, kv,
        (o_own, o_other),
        (lse_own.astype(jnp.float32), lse_other.astype(jnp.float32)),
        (first_of_doc(ctx), first_of_doc(ctx ^ 1)),
    )
    f32, bf16 = jnp.float32, jnp.bfloat16
    dq_send = [(a + swap_cores(b).astype(f32)).astype(bf16) for a, b in zip(dq_own, dq_other)]
    back = dkv_far[planes - 1]
    for plane in range(planes - 1, 0, -1):
        moved = [rotate_ctx(x, -2) for x in back]
        back = [(a.astype(f32) + b.astype(f32)).astype(bf16) for a, b in zip(moved, dkv_far[plane - 1])]
    back = [rotate_ctx(x, -2) for x in back]
    dkv_send = [(a + b.astype(f32)).astype(bf16) for a, b in zip(dkv_own, back)]
    dq_back = xor_order(jnp.stack(exchange(dq_send)), head)
    dkv_back = xor_order(jnp.stack(exchange(dkv_send)), head)
    dq = jnp.transpose(dq_back, (2, 0, 1, 3)).reshape(rows, heads_all, width)
    dk = jnp.transpose(dkv_back[:, 0], (2, 0, 1, 3)).reshape(rows, kv_all, width)
    dv = jnp.transpose(dkv_back[:, 1], (2, 0, 1, 3)).reshape(rows, kv_all, width)
    return dq, dk, dv


def solution(mesh):
    return jax.shard_map(
        per_device,
        mesh=mesh,
        in_specs=(
            P(("ctx", "head"), None, None),
            P(("ctx", "head"), None, None),
            P(("ctx", "head"), None, None),
            P("ctx", "head", None),
            P(("ctx", "head"), None, None),
            P("head", "ctx"),
            P(),
        ),
        out_specs=(
            P(("ctx", "head"), None, None),
            P(("ctx", "head"), None, None),
            P(("ctx", "head"), None, None),
        ),
        check_vma=False,
    )
```

```python
import functools
import math

import jax
import jax.numpy as jnp
from jax import lax
from jax.experimental import pallas as pl
from jax.experimental.pallas import tpu as pltpu
from jax.sharding import PartitionSpec as P

soft_cap = 50.0
score_scale = 144.0 ** (-0.5)
log2e = math.log2(math.e)


def swap_heads(value, step):
    count = lax.axis_size("head")
    return lax.ppermute(value, "head", [(i, i ^ step) for i in range(count)])


def rotate_ctx(value, steps):
    count = lax.axis_size("ctx")
    return lax.ppermute(value, "ctx", [(i, (i + steps) % count) for i in range(count)])


def swap_cores(value):
    count = lax.axis_size("ctx")
    return lax.ppermute(value, "ctx", [(i, i ^ 1) for i in range(count)])


def xor_order(blocks, index):
    count = blocks.shape[0]
    step = 1
    while step < count:
        swapped = blocks.reshape((count // (2 * step), 2, step) + blocks.shape[1:])[:, ::-1].reshape(blocks.shape)
        blocks = jnp.where((index & step) != 0, swapped, blocks)
        step *= 2
    return blocks


def dot(a, b, contract):
    return lax.dot_general(a, b, ((contract[0], contract[1]), ((), ())), preferred_element_type=jnp.float32)

NT = ((1,), (1,))
NN = ((1,), (0,))

def grads_kernel(planes, far, group, n_pieces, *refs):
    refs = list(refs)

    def take(n):
        out = refs[:n]
        del refs[:n]
        return out

    own_q, other_q = take(n_pieces), take(n_pieces)
    kv = [take(n_pieces) for _ in range(planes + 1)]
    own_o, other_o, own_lse, other_lse, own_start, other_start = take(6)
    dq_own, dq_other = take(n_pieces), take(n_pieces)
    dkv = [take(n_pieces) for _ in range(planes + 1)]
    (mask_ref,) = take(1)

    kv_heads, rows, width = kv[0][0].shape[1:]
    keys = rows * n_pieces
    ctx = lax.axis_index("ctx")
    head = lax.axis_index("head")
    core = ctx & 1
    tasks = [(0, plane) for plane in range(planes + 1)]
    tasks += [(1, plane) for plane in range(planes) if 2 * plane + 1 <= far]

    row = lax.broadcasted_iota(jnp.int32, (keys, 1), 0)
    lane = lax.broadcasted_iota(jnp.int32, (1, keys), 1)
    spot = lambda x: ((x // rows) ^ head) * rows + x % rows
    for n, (which, plane) in enumerate(tasks):
        start = (own_start, other_start)[which][...]
        behind = 2 * plane if which == 0 else 2 * (plane + core)
        k_pos = (ctx - behind) * keys + spot(row)
        allowed = k_pos >= start
        if which == 0 and plane == 0:
            allowed = allowed & (k_pos <= ctx * keys + spot(lane))
        mask_ref[n] = jnp.where(allowed, 1.0, 0.0)

    def one_head(i, carry):
        ones = jnp.ones((8, width), jnp.bfloat16)
        q_sets = []
        for pieces, o_ref, lse_ref in ((own_q, own_o, own_lse), (other_q, other_o, other_lse)):
            per_head = []
            for g in range(group):
                h = i * group + g
                q_rows = jnp.concatenate([piece[0, h] for piece in pieces], axis=0)
                g_rows = jnp.concatenate([piece[1, h] for piece in pieces], axis=0)
                prod = g_rows.astype(jnp.float32) * o_ref[h].astype(jnp.float32)
                high = prod.astype(jnp.bfloat16)
                low = (prod - high.astype(jnp.float32)).astype(jnp.bfloat16)
                delta = (dot(ones, high, NT) + dot(ones, low, NT))[0:1]
                per_head.append((q_rows, g_rows, delta, lse_ref[i, :, g * keys : (g + 1) * keys] * log2e))
            q_sets.append(per_head)
        k_all, v_all = [], []
        for plane in range(planes + 1):
            k_all.append(jnp.concatenate([piece[0, i] for piece in kv[plane]], axis=0))
            v_all.append(jnp.concatenate([piece[1, i] for piece in kv[plane]], axis=0))
        dk = [None] * (planes + 1)
        dv = [None] * (planes + 1)
        dq = [[None] * group, [None] * group]
        add = lambda a, b: b if a is None else a + b
        for n, (which, plane) in enumerate(tasks):
            if which == 0:
                k_rows, v_rows = k_all[plane], v_all[plane]
            else:
                k_rows = jnp.where(core == 0, k_all[plane], k_all[plane + 1])
                v_rows = jnp.where(core == 0, v_all[plane], v_all[plane + 1])
            k_turned = k_rows.T
            dk_part = dv_part = None
            for g in range(group):
                q_rows, g_rows, delta, lse2 = q_sets[which][g]
                t = jnp.tanh(dot(k_rows, q_rows, NT) * (score_scale / soft_cap))
                weights = jnp.exp2(t * (soft_cap * log2e) - lse2) * mask_ref[n]
                d_scores = (weights * (dot(v_rows, g_rows, NT) - delta)) * (1.0 - t * t)
                d_scores = d_scores.astype(jnp.bfloat16)
                dk_part = add(dk_part, dot(d_scores, q_rows, NN))
                dv_part = add(dv_part, dot(weights.astype(jnp.bfloat16), g_rows, NN))
                dq[which][g] = add(dq[which][g], dot(k_turned, d_scores, NN))
            if which == 0:
                dk[plane], dv[plane] = dk_part, dv_part
            else:
                for side in range(2):
                    chosen = core == side
                    dk[plane + side] = dk[plane + side] + jnp.where(chosen, dk_part, 0.0)
                    dv[plane + side] = dv[plane + side] + jnp.where(chosen, dv_part, 0.0)
        for which, outs in ((0, dq_own), (1, dq_other)):
            for g in range(group):
                full = (dq[which][g] * score_scale).T
                for p in range(n_pieces):
                    outs[p][i * group + g] = full[p * rows : (p + 1) * rows].astype(outs[p].dtype)
        for plane in range(planes + 1):
            for p in range(n_pieces):
                span = slice(p * rows, (p + 1) * rows)
                dkv[plane][p][0, i] = (dk[plane][span] * score_scale).astype(dkv[plane][p].dtype)
                dkv[plane][p][1, i] = dv[plane][span].astype(dkv[plane][p].dtype)
        return carry

    lax.fori_loop(0, kv_heads, one_head, 0, unroll=min(2, kv_heads))


def grads_call(planes, far, group, own_q, other_q, kv, o_pair, lse_pair, start_pair):
    n_pieces = len(own_q)
    _, heads, rows, width = own_q[0].shape
    kv_heads = heads // group
    keys = rows * n_pieces
    f32, bf16 = jnp.float32, jnp.bfloat16
    shape = jax.ShapeDtypeStruct
    dq_shape, kv_shape = (heads, rows, width), (2, kv_heads, rows, width)
    pairs = kv_heads * (2 * planes + 1) * group
    n_in = (planes + 3) * n_pieces + 6
    n_out = (planes + 3) * n_pieces
    vmem = pl.BlockSpec(memory_space=pltpu.VMEM)
    outs = pl.pallas_call(
        functools.partial(grads_kernel, planes, far, group, n_pieces),
        in_specs=[vmem] * n_in,
        out_specs=[vmem] * n_out,
        out_shape=[shape(dq_shape, f32)] * n_pieces
        + [shape(dq_shape, bf16)] * n_pieces
        + [shape(kv_shape, f32)] * n_pieces
        + [shape(kv_shape, bf16)] * (planes * n_pieces),
        scratch_shapes=[pltpu.VMEM((2 * planes + 1, keys, keys), f32)],
        compiler_params=pltpu.CompilerParams(vmem_limit_bytes=32 * 1024 * 1024),
        cost_estimate=pl.CostEstimate(
            flops=pairs * 10 * keys * keys * width, bytes_accessed=8 * 1024 * 1024, transcendentals=pairs * 2 * keys * keys
        ),
        name="grads",
    )(*own_q, *other_q, *[piece for plane in kv for piece in plane], *o_pair, *lse_pair, *start_pair)
    chunks = [outs[i : i + n_pieces] for i in range(0, len(outs), n_pieces)]
    return chunks[0], chunks[1], chunks[2], chunks[3:]


def per_device(query, key, value, attn_out, out_grad, lse, doc_lengths):
    n_ctx, n_head = lax.axis_size("ctx"), lax.axis_size("head")
    far = min(6, n_ctx // 4)
    planes = (far + 1) // 2
    rows, heads_all, width = query.shape
    kv_all = key.shape[1]
    group = heads_all // kv_all
    ctx, head = lax.axis_index("ctx"), lax.axis_index("head")

    def piece(arrays, p):
        parts = []
        for x in arrays:
            blocks = x.reshape(rows, n_head, x.shape[1] // n_head, width)
            part = lax.dynamic_index_in_dim(blocks, head ^ p, 1, keepdims=False)
            parts.append(jnp.transpose(part, (1, 0, 2)))
        return jnp.stack(parts)

    kv_send = [piece((key, value), p) for p in range(n_head)]
    q_send = [piece((query, out_grad), p) for p in range(n_head)]
    exchange = lambda pieces: [pieces[0]] + [swap_heads(pieces[p], p) for p in range(1, n_head)]
    kv_own = exchange(kv_send)
    q_own = exchange(q_send)
    kv = [kv_own]
    for _ in range(planes):
        kv.append([rotate_ctx(piece_, 2) for piece_ in kv[-1]])
    q_other = [swap_cores(piece_) for piece_ in q_own]

    tok = rows * n_head
    heads_here = attn_out.shape[1]
    o_blocks = xor_order(attn_out.reshape(n_head, rows, heads_here, width), head)
    o_own = jnp.transpose(o_blocks, (2, 0, 1, 3)).reshape(heads_here, tok, width)
    o_other = swap_cores(o_own)
    lse_blocks = xor_order(jnp.transpose(lse.reshape(heads_here, n_head, rows), (1, 0, 2)), head)
    lse_own = jnp.transpose(lse_blocks, (1, 0, 2)).reshape(heads_here // group, 1, group * tok)
    lse_other = swap_cores(lse_own)

    doc_ends = jnp.cumsum(doc_lengths)

    def first_of_doc(block):
        lane = jnp.arange(tok, dtype=jnp.int32)
        pos = block * tok + ((lane // rows) ^ head) * rows + lane % rows
        start = jnp.max(jnp.where(doc_ends[None, :] <= pos[:, None], doc_ends[None, :], 0), axis=1)
        return start[None]

    dq_own, dq_other, dkv_own, dkv_far = grads_call(
        planes, far, group, q_own, q_other, kv,
        (o_own, o_other),
        (lse_own.astype(jnp.float32), lse_other.astype(jnp.float32)),
        (first_of_doc(ctx), first_of_doc(ctx ^ 1)),
    )
    f32, bf16 = jnp.float32, jnp.bfloat16
    dq_send = [(a + swap_cores(b).astype(f32)).astype(bf16) for a, b in zip(dq_own, dq_other)]
    back = dkv_far[planes - 1]
    for plane in range(planes - 1, 0, -1):
        moved = [rotate_ctx(x, -2) for x in back]
        back = [(a.astype(f32) + b.astype(f32)).astype(bf16) for a, b in zip(moved, dkv_far[plane - 1])]
    back = [rotate_ctx(x, -2) for x in back]
    dkv_send = [(a + b.astype(f32)).astype(bf16) for a, b in zip(dkv_own, back)]
    dq_back = xor_order(jnp.stack(exchange(dq_send)), head)
    dkv_back = xor_order(jnp.stack(exchange(dkv_send)), head)
    dq = jnp.transpose(dq_back, (2, 0, 1, 3)).reshape(rows, heads_all, width)
    dk = jnp.transpose(dkv_back[:, 0], (2, 0, 1, 3)).reshape(rows, kv_all, width)
    dv = jnp.transpose(dkv_back[:, 1], (2, 0, 1, 3)).reshape(rows, kv_all, width)
    return dq, dk, dv


def solution(mesh):
    return jax.shard_map(
        per_device,
        mesh=mesh,
        in_specs=(
            P(("ctx", "head"), None, None),
            P(("ctx", "head"), None, None),
            P(("ctx", "head"), None, None),
            P("ctx", "head", None),
            P(("ctx", "head"), None, None),
            P("head", "ctx"),
            P(),
        ),
        out_specs=(
            P(("ctx", "head"), None, None),
            P(("ctx", "head"), None, None),
            P(("ctx", "head"), None, None),
        ),
        check_vma=False,
    )
```
